32 devices in a mesh: groups: 2 (over x), dp: 8 (over z, y), tensor: 2 (over core).
Axes of the slice: x: 2, y: 2, z: 4, core: 2. Of those that a mesh axis runs over, the one named last changes fastest.
Arguments:
- activations: bfloat16 [8192, 8192], P(('groups', 'dp'), 'tensor'), parts along dimension 0, may hold values from -6 to 6
- gradients: bfloat16 [8192, 14336], P(('groups', 'dp'), 'tensor'), parts along dimension 0, may hold values from -6 to 6
- basis_in: bfloat16 [8, 1024, 1024], P('tensor', None, 'dp'), may hold values from -0.1875 to 0.1875
- basis_out: bfloat16 [14, 1024, 1024], P('tensor', None, 'dp'), may hold values from -0.1875 to 0.1875
- eigen_in: float32 [8, 1024], P('tensor'), may hold values from 0.01 to 10
- eigen_out: float32 [14, 1024], P('tensor'), may hold values from 0.01 to 10
- query_in: bfloat16 [128, 8192], P('dp', 'tensor'), may hold values from -0.0625 to 0.0625
- query_out: bfloat16 [128, 14336], P('dp', 'tensor'), may hold values from -0.046875 to 0.046875
Outputs:
- scores: float32 [8192, 32], P(('groups', 'dp')), parts along dimension 0
The draws below stay inside these ranges and needn't reach their ends.
There are 2 independent parts, one for each index of `groups`. The reference program is written for one: setup_inputs(seed, part) draws one part's arguments, and reference() takes and returns one part's arrays. A program takes and returns all parts, laid end to end along the dimension named above; an argument that names none is the same for every part. Nothing has to cross between parts.
All inputs are finite; a program needn't handle non-finite values.
Results may differ from the reference program's by a relative error of at most 0.0003.
Values may be sent and summed in bfloat16 or wider, within the bound.
A program may use at most 128 MiB of HBM per device.

```python
import math
import jax
import jax.numpy as jnp
from jax import lax

WIDTH = 8192
HIDDEN_SIZE = 14336
BLOCK = 1024
QUERIES = 32
FACTORS = 4
TOK_DEV = 512
QROWS = 128
NB_IN = 8
NB_OUT = 14
TOKENS = 4096
N_DP = 8


def shard_levels(key, shape, split, smallest, largest):
    def one(dim, blocks):
        heights = jax.random.uniform(jax.random.fold_in(jax.random.fold_in(key, 6), dim), (blocks,), jnp.float32, smallest / len(split), largest / len(split))
        return jnp.repeat(jnp.exp(heights), shape[dim] // blocks).reshape((-1,) + (1,) * (len(shape) - dim - 1))

    factor_of = one(*split[0])
    for cut in split[1:]:
        factor_of = factor_of * one(*cut)
    return factor_of


def bell_draw(stream_key, extent, spread, limit, pieces=(), held_as=jnp.bfloat16):
    array = spread * jax.random.normal(stream_key, extent, jnp.float32)
    if pieces:
        array = array * shard_levels(stream_key, extent, pieces, -0.22, 0.18)
    return jnp.clip(array, -limit, limit).astype(held_as)


def setup_inputs(seed: int = 0, part: int = 0) -> dict:
    key_list = jax.random.split(jax.random.key(seed), 9)
    part_splits = jax.random.split(jax.random.fold_in(key_list[8], part), 9)
    activations = bell_draw(part_splits[0], (TOKENS, WIDTH), 1.0, 6.0, ((0, 8), (1, 2)))
    gradients = bell_draw(part_splits[1], (TOKENS, HIDDEN_SIZE), 1.0, 6.0, ((0, 8), (1, 2)))
    basis_in = bell_draw(key_list[2], (NB_IN, BLOCK, BLOCK), BLOCK ** -0.5, 0.1875, ((0, 2), (2, 8)))
    basis_out = bell_draw(key_list[3], (NB_OUT, BLOCK, BLOCK), BLOCK ** -0.5, 0.1875, ((0, 2), (2, 8)))
    eigen_in = jnp.clip(jnp.exp(math.log(10.0) - 6.9077553 * jax.random.uniform(key_list[4], (NB_IN, BLOCK), jnp.float32) ** shard_levels(key_list[4], (NB_IN, BLOCK), ((0, 2),), -0.2, 0.2)), 0.01, 10.0)
    eigen_out = jnp.clip(jnp.exp(math.log(10.0) - 6.9077553 * jax.random.uniform(key_list[5], (NB_OUT, BLOCK), jnp.float32) ** shard_levels(key_list[5], (NB_OUT, BLOCK), ((0, 2),), -0.2, 0.2)), 0.01, 10.0)
    query_in = bell_draw(key_list[6], (QROWS, WIDTH), WIDTH ** -0.5, 0.0625, ((0, 8), (1, 2)))
    query_out = bell_draw(key_list[7], (QROWS, HIDDEN_SIZE), HIDDEN_SIZE ** -0.5, 0.046875, ((0, 8), (1, 2)))
    return dict(activations=activations, gradients=gradients, basis_in=basis_in, basis_out=basis_out, eigen_in=eigen_in, eigen_out=eigen_out, query_in=query_in, query_out=query_out)


damping = 0.1

def carried_back(basis, eigen, query):
    scale = 1.0 / jnp.sqrt(eigen + damping)
    blocks = basis.shape[0]
    weighted = query.astype(jnp.float32).reshape(QROWS, blocks, BLOCK) * scale[None]
    back = jnp.einsum('bij,qbj->qbi', basis.astype(jnp.float32), weighted, precision=lax.Precision.HIGHEST)
    return back.reshape(QROWS, blocks * BLOCK)

def reference(activations, gradients, basis_in, basis_out, eigen_in, eigen_out, query_in, query_out):
    back_in = carried_back(basis_in, eigen_in, query_in)
    back_out = carried_back(basis_out, eigen_out, query_out)
    act_blocks = activations.reshape(N_DP, TOK_DEV, WIDTH)
    grad_blocks = gradients.reshape(N_DP, TOK_DEV, HIDDEN_SIZE)

    def one_block(pair):
        part_in = jnp.dot(pair[0].astype(jnp.float32), back_in.T, precision=lax.Precision.HIGHEST)
        part_out = jnp.dot(pair[1].astype(jnp.float32), back_out.T, precision=lax.Precision.HIGHEST)
        return lax.optimization_barrier(jnp.sum((part_in * part_out).reshape(TOK_DEV, QUERIES, FACTORS), axis=2))
    scores = lax.map(one_block, (act_blocks, grad_blocks))
    return scores.reshape(TOKENS, QUERIES)
```

```python
import jax
import jax.numpy as jnp
from jax import lax
from jax.sharding import PartitionSpec as P

FACTORS = 4
damping = 0.1


def split(x):
    hi = lax.reduce_precision(x, 8, 7)
    return hi.astype(jnp.bfloat16), (x - hi).astype(jnp.bfloat16)


def make(mesh):
    groups, dp = mesh.shape["groups"], mesh.shape["dp"]

    def on_device(
        activations, gradients, basis_in, basis_out, eigen_in, eigen_out, query_in, query_out
    ):
        g, d = lax.axis_index("groups"), lax.axis_index("dp")
        rows = query_in.shape[0] // groups
        tokens = activations.shape[0]

        def mine(query, eigen):
            blocks, width = eigen.shape
            part = lax.dynamic_slice_in_dim(query, g * rows, rows, 0)
            return part.reshape(rows, blocks, dp, width // dp)

        sent = jnp.concatenate([mine(query_in, eigen_in), mine(query_out, eigen_out)], 1)
        got = lax.all_to_all(sent.transpose(2, 0, 1, 3), "dp", 0, 0)
        cols = got.shape[3]
        blocks = got.shape[2]
        eigen = jnp.concatenate([eigen_in, eigen_out], 0)
        scale = 1.0 / jnp.sqrt(lax.dynamic_slice_in_dim(eigen, d * cols, cols, 1) + damping)
        weighted = got.reshape(dp * rows, blocks, cols).astype(jnp.float32) * scale[None]
        both = jnp.concatenate(split(weighted), 0)
        n_in = basis_in.shape[0]

        def back(basis, w):
            y = jnp.einsum("qbj,bij->qbi", w, basis, preferred_element_type=jnp.float32)
            return y[: dp * rows] + y[dp * rows :]

        partial = jnp.concatenate(
            [back(basis_in, both[:, :n_in]), back(basis_out, both[:, n_in:])], 1
        )
        own = lax.psum_scatter(partial, "dp", scatter_dimension=0, tiled=True)
        full = lax.all_gather(own, ("groups", "dp"), axis=0, tiled=True)
        total = full.shape[0]
        hl = jnp.concatenate(split(full), 0)

        def project(x, m):
            y = lax.dot_general(
                x, m.reshape(2 * total, -1), (((1,), (1,)), ((), ())), preferred_element_type=jnp.float32
            )
            return y[:, :total] + y[:, total:]

        part_in = project(activations, hl[:, :n_in])
        part_out = project(gradients, hl[:, n_in:])
        part_in, part_out = lax.psum((part_in, part_out), "tensor")
        products = (part_in * part_out).reshape(tokens, groups, dp, rows).transpose(0, 2, 1, 3)
        return jnp.sum(products.reshape(tokens, total // FACTORS, FACTORS), axis=2)

    return on_device


def solution(mesh):
    placed = (
        P(("groups", "dp"), "tensor"),
        P(("groups", "dp"), "tensor"),
        P("tensor", None, "dp"),
        P("tensor", None, "dp"),
        P("tensor", None),
        P("tensor", None),
        P("dp", "tensor"),
        P("dp", "tensor"),
    )
    return jax.shard_map(
        make(mesh), mesh=mesh, in_specs=placed, out_specs=P(("groups", "dp"), None), check_vma=False
    )
```

```python
import functools

import jax
import jax.numpy as jnp
from jax import lax
from jax.experimental import pallas as pl
from jax.experimental.pallas import tpu as pltpu
from jax.sharding import PartitionSpec as P

FACTORS = 4
LANES = 128
damping = 0.1

SPAN = 240.0


def split(x):
    hi = lax.reduce_precision(x, 8, 7)
    return hi.astype(jnp.bfloat16), (x - hi).astype(jnp.bfloat16)


def encode(x):
    bound = lax.reduce_precision(jnp.maximum(jnp.max(jnp.abs(x), axis=-1), 1e-30) * 1.01, 8, 7)
    y = jnp.exp2(jnp.abs(x) * (SPAN / bound)[..., None] - SPAN / 2)
    code = jnp.where(x < 0, -y, y).astype(jnp.bfloat16)
    tail = jnp.pad(bound, [(0, 0)] * (bound.ndim - 1) + [(0, LANES - bound.shape[-1])])
    return jnp.concatenate(
        [code.reshape(*x.shape[:-2], -1), tail.astype(jnp.bfloat16)], axis=-1
    )


def decode(code, bound):
    c = code.astype(jnp.float32)
    size = (jnp.log2(jnp.abs(c)) + SPAN / 2) * (bound * (1.0 / SPAN))
    return jnp.where(c < 0, -size, size)


def project_kernel(first, x_ref, code_ref, bound_ref, out_ref):
    b = pl.program_id(0)
    bounds = bound_ref[...].astype(jnp.float32)
    lane = lax.broadcasted_iota(jnp.int32, bounds.shape, 1)
    bound = jnp.sum(jnp.where(lane == b + first, bounds, 0.0), axis=1, keepdims=True)
    value = decode(code_ref[...], bound)
    hi = value.astype(jnp.bfloat16)
    lo = (value - hi.astype(jnp.float32)).astype(jnp.bfloat16)
    y = lax.dot_general(
        x_ref[...],
        jnp.concatenate([hi, lo], axis=0),
        (((1,), (1,)), ((), ())),
        preferred_element_type=jnp.float32,
    )
    total = code_ref.shape[0]
    y = y[:, :total] + y[:, total:]

    @pl.when(b == 0)
    def _():
        out_ref[...] = y

    @pl.when(b > 0)
    def _():
        out_ref[...] += y


def project(x, codes, first, blocks, all_blocks):
    tokens, width = x.shape[0], x.shape[1] // blocks
    total = codes.shape[0]
    return pl.pallas_call(
        functools.partial(project_kernel, first),
        grid=(blocks,),
        out_shape=jax.ShapeDtypeStruct((tokens, total), jnp.float32),
        in_specs=[
            pl.BlockSpec((tokens, width), lambda b: (0, b)),
            pl.BlockSpec((total, width), lambda b: (0, b + first)),
            pl.BlockSpec((total, LANES), lambda b: (0, all_blocks * width // LANES)),
        ],
        out_specs=pl.BlockSpec((tokens, total), lambda b: (0, 0)),
        cost_estimate=pl.CostEstimate(
            flops=4 * tokens * total * width * blocks,
            bytes_accessed=2 * (tokens + total) * width * blocks,
            transcendentals=total * width * blocks,
        ),
    )(x, codes, codes)


def swap_rows(codes, mesh):
    return lax.all_to_all(codes, "dp", 0, 0)


def gather_rows(own, mesh):
    return lax.all_gather(own, ("groups", "dp"), axis=0, tiled=True)


def make(mesh):
    groups, dp = mesh.shape["groups"], mesh.shape["dp"]

    def on_device(
        activations, gradients, basis_in, basis_out, eigen_in, eigen_out, query_in, query_out
    ):
        g, d = lax.axis_index("groups"), lax.axis_index("dp")
        rows = query_in.shape[0] // groups
        tokens = activations.shape[0]
        n_in, n_out = basis_in.shape[0], basis_out.shape[0]
        blocks, width, cols = n_in + n_out, basis_in.shape[1], basis_in.shape[2]

        def mine(query, count):
            part = lax.dynamic_slice_in_dim(query, g * rows, rows, 0)
            return part.reshape(rows, count, dp, cols)

        sent = jnp.concatenate([mine(query_in, n_in), mine(query_out, n_out)], 1)
        got = lax.all_to_all(sent.transpose(2, 0, 1, 3), "dp", 0, 0)
        eigen = jnp.concatenate([eigen_in, eigen_out], 0)
        scale = 1.0 / jnp.sqrt(lax.dynamic_slice_in_dim(eigen, d * cols, cols, 1) + damping)
        weighted = got.reshape(dp * rows, blocks, cols).astype(jnp.float32) * scale[None]
        both = jnp.concatenate(split(weighted), 0)

        def back(basis, w):
            y = jnp.einsum("qbj,bij->qbi", w, basis, preferred_element_type=jnp.float32)
            return y[: dp * rows] + y[dp * rows :]

        partial = jnp.concatenate(
            [back(basis_in, both[:, :n_in]), back(basis_out, both[:, n_in:])], 1
        )
        codes = swap_rows(encode(partial.reshape(dp, rows, blocks, width)), mesh)
        bounds = codes[..., blocks * width : blocks * width + blocks].astype(jnp.float32)
        parts = codes[..., : blocks * width].reshape(dp, rows, blocks, width)
        own = jnp.sum(decode(parts, bounds[..., None]), axis=0)
        full = gather_rows(encode(own), mesh)
        total = groups * dp * rows
        full = full.reshape(total, -1)
        part_in = project(activations, full, 0, n_in, blocks)
        part_out = project(gradients, full, n_in, n_out, blocks)
        part_in, part_out = lax.psum((part_in, part_out), "tensor")
        products = (part_in * part_out).reshape(tokens, groups, dp, rows).transpose(0, 2, 1, 3)
        return jnp.sum(products.reshape(tokens, total // FACTORS, FACTORS), axis=2)

    return on_device


def solution(mesh):
    placed = (
        P(("groups", "dp"), "tensor"),
        P(("groups", "dp"), "tensor"),
        P("tensor", None, "dp"),
        P("tensor", None, "dp"),
        P("tensor", None),
        P("tensor", None),
        P("dp", "tensor"),
        P("dp", "tensor"),
    )
    return jax.shard_map(
        make(mesh), mesh=mesh, in_specs=placed, out_specs=P(("groups", "dp"), None), check_vma=False
    )
```

```python
import functools

import jax
import jax.numpy as jnp
from jax import lax
from jax.experimental import pallas as pl
from jax.experimental.pallas import tpu as pltpu
from jax.sharding import PartitionSpec as P

FACTORS = 4
LANES = 128
damping = 0.1

SPAN = 240.0


def split(x):
    hi = lax.reduce_precision(x, 8, 7)
    return hi.astype(jnp.bfloat16), (x - hi).astype(jnp.bfloat16)


def encode(x):
    bound = lax.reduce_precision(jnp.maximum(jnp.max(jnp.abs(x), axis=-1), 1e-30) * 1.01, 8, 7)
    y = jnp.exp2(jnp.abs(x) * (SPAN / bound)[..., None] - SPAN / 2)
    code = jnp.where(x < 0, -y, y).astype(jnp.bfloat16)
    tail = jnp.pad(bound, [(0, 0)] * (bound.ndim - 1) + [(0, LANES - bound.shape[-1])])
    return jnp.concatenate(
        [code.reshape(*x.shape[:-2], -1), tail.astype(jnp.bfloat16)], axis=-1
    )


def decode(code, bound):
    c = code.astype(jnp.float32)
    size = (jnp.log2(jnp.abs(c)) + SPAN / 2) * (bound * (1.0 / SPAN))
    return jnp.where(c < 0, -size, size)


def project_kernel(first, x_ref, code_ref, bound_ref, out_ref):
    b = pl.program_id(0)
    bounds = bound_ref[...].astype(jnp.float32)
    lane = lax.broadcasted_iota(jnp.int32, bounds.shape, 1)
    bound = jnp.sum(jnp.where(lane == b + first, bounds, 0.0), axis=1, keepdims=True)
    value = decode(code_ref[...], bound)
    hi = value.astype(jnp.bfloat16)
    lo = (value - hi.astype(jnp.float32)).astype(jnp.bfloat16)
    y = lax.dot_general(
        x_ref[...],
        jnp.concatenate([hi, lo], axis=0),
        (((1,), (1,)), ((), ())),
        preferred_element_type=jnp.float32,
    )
    total = code_ref.shape[0]
    y = y[:, :total] + y[:, total:]

    @pl.when(b == 0)
    def _():
        out_ref[...] = y

    @pl.when(b > 0)
    def _():
        out_ref[...] += y


def project(x, codes, first, blocks, all_blocks):
    tokens, width = x.shape[0], x.shape[1] // blocks
    total = codes.shape[0]
    return pl.pallas_call(
        functools.partial(project_kernel, first),
        grid=(blocks,),
        out_shape=jax.ShapeDtypeStruct((tokens, total), jnp.float32),
        in_specs=[
            pl.BlockSpec((tokens, width), lambda b: (0, b)),
            pl.BlockSpec((total, width), lambda b: (0, b + first)),
            pl.BlockSpec((total, LANES), lambda b: (0, all_blocks * width // LANES)),
        ],
        out_specs=pl.BlockSpec((tokens, total), lambda b: (0, 0)),
        cost_estimate=pl.CostEstimate(
            flops=4 * tokens * total * width * blocks,
            bytes_accessed=2 * (tokens + total) * width * blocks,
            transcendentals=total * width * blocks,
        ),
    )(x, codes, codes)


def swap_rows(codes, mesh):
    return lax.all_to_all(codes, "dp", 0, 0)


MESH = pl.DeviceIdType.MESH


def gather_kernel(groups, lines, pairs, own_ref, out_ref, local_sem, send_sem, recv_sem):
    g, d = lax.axis_index("groups"), lax.axis_index("dp")
    t = lax.axis_index("tensor")
    a, b = d // pairs, d % pairs
    length = own_ref.shape[1]
    middle = (length // LANES + 1) // 2 * LANES
    halves = (pl.ds(0, middle), pl.ds(middle, length - middle))
    order = [k for pair in zip(range(1, lines), range(lines - 1, 0, -1)) for k in pair]
    order = list(dict.fromkeys(order))
    line_peers = [(g, (a + k) % lines * pairs + b, t) for k in order]
    pair_peers = [(g, a * pairs + (b + k) % pairs, t) for k in range(1, pairs)]
    group_peers = [((g + k) % groups, d, t) for k in range(1, groups)]
    other_b = [(b + k) % pairs for k in range(1, pairs)]
    other_g = [(g + k) % groups for k in range(1, groups)]

    barrier = pltpu.get_barrier_semaphore()
    peers = line_peers + pair_peers + group_peers
    for peer in peers:
        pl.semaphore_signal(barrier, inc=1, device_id=peer, device_id_type=MESH)
    pl.semaphore_wait(barrier, len(peers))

    started = []

    def send(pg, pd, half, peer, own=False):
        src = own_ref.at[:, halves[half]] if own else out_ref.at[pg, pd, :, halves[half]]
        copy = pltpu.make_async_remote_copy(
            src_ref=src,
            dst_ref=out_ref.at[pg, pd, :, halves[half]],
            send_sem=send_sem.at[len(started)],
            recv_sem=recv_sem.at[pg, pd, half],
            device_id=peer,
            device_id_type=MESH,
        )
        copy.start()
        started.append(copy)

    def arrived(pg, pd, half):
        here = out_ref.at[pg, pd, :, halves[half]]
        pltpu.make_async_remote_copy(
            src_ref=here,
            dst_ref=here,
            send_sem=send_sem.at[0],
            recv_sem=recv_sem.at[pg, pd, half],
            device_id=peers[0],
            device_id_type=MESH,
        ).wait_recv()

    def across(pa):
        for ob in other_b:
            arrived(g, pa * pairs + ob, 0)
            for peer in group_peers:
                send(g, pa * pairs + ob, 0, peer)
        for og in other_g:
            arrived(og, pa * pairs + b, 1)
            for peer in pair_peers:
                send(og, pa * pairs + b, 1, peer)

    for half in (0, 1):
        for peer in line_peers:
            send(g, d, half, peer, True)
        for peer in pair_peers + group_peers:
            send(g, d, half, peer, True)
    local = pltpu.make_async_copy(own_ref, out_ref.at[g, d], local_sem)
    local.start()
    places = [a] + [(a - k) % lines for k in order]
    for i, pa in enumerate(places):
        if i > 0:
            for half in (0, 1):
                arrived(g, pa * pairs + b, half)
                for peer in pair_peers + group_peers:
                    send(g, pa * pairs + b, half, peer)
            across(places[i - 1])
    across(places[-1])
    for pa in places:
        for ob in other_b:
            arrived(g, pa * pairs + ob, 1)
        for og in other_g:
            arrived(og, pa * pairs + b, 0)
            for ob in other_b:
                for half in (0, 1):
                    arrived(og, pa * pairs + ob, half)
    local.wait()
    for copy in started:
        copy.wait_send()


def gather_rows(own, mesh):
    groups, dp = mesh.shape["groups"], mesh.shape["dp"]
    pairs = 2 if dp % 2 == 0 else 1
    lines = dp // pairs
    cross = (pairs - 1) + (groups - 1)
    sends = 2 * (lines - 1) + 2 * lines * cross + 2 * lines * (pairs - 1) * (groups - 1)
    vmem = pl.BlockSpec(memory_space=pltpu.VMEM)
    return pl.pallas_call(
        functools.partial(gather_kernel, groups, lines, pairs),
        out_shape=jax.ShapeDtypeStruct((groups, dp, *own.shape), own.dtype),
        in_specs=[vmem],
        out_specs=vmem,
        scratch_shapes=[
            pltpu.SemaphoreType.DMA,
            pltpu.SemaphoreType.DMA((sends,)),
            pltpu.SemaphoreType.DMA((groups, dp, 2)),
        ],
        compiler_params=pltpu.CompilerParams(collective_id=0, has_side_effects=True),
    )(own)


def product_kernel(in_ref, out_part_ref, prod_ref, held, send_sem, recv_sem):
    other = (lax.axis_index("groups"), lax.axis_index("dp"), 1 - lax.axis_index("tensor"))
    barrier = pltpu.get_barrier_semaphore()
    pl.semaphore_signal(barrier, inc=1, device_id=other, device_id_type=MESH)
    pl.semaphore_wait(barrier, 1)
    copies = []
    for i, ref in enumerate((in_ref, out_part_ref)):
        copy = pltpu.make_async_remote_copy(
            src_ref=ref,
            dst_ref=held.at[i],
            send_sem=send_sem.at[i],
            recv_sem=recv_sem.at[i],
            device_id=other,
            device_id_type=MESH,
        )
        copy.start()
        copies.append(copy)
    for copy in copies:
        copy.wait()
    prod_ref[...] = (in_ref[...] + held[0]) * (out_part_ref[...] + held[1])


def product(part_in, part_out, mesh):
    if mesh.shape["tensor"] != 2:
        part_in, part_out = lax.psum((part_in, part_out), "tensor")
        return part_in * part_out
    vmem = pl.BlockSpec(memory_space=pltpu.VMEM)
    return pl.pallas_call(
        product_kernel,
        out_shape=jax.ShapeDtypeStruct(part_in.shape, part_in.dtype),
        in_specs=[vmem, vmem],
        out_specs=vmem,
        scratch_shapes=[
            pltpu.VMEM((2, *part_in.shape), part_in.dtype),
            pltpu.SemaphoreType.DMA((2,)),
            pltpu.SemaphoreType.DMA((2,)),
        ],
        compiler_params=pltpu.CompilerParams(collective_id=1, has_side_effects=True),
    )(part_in, part_out)


def make(mesh):
    groups, dp = mesh.shape["groups"], mesh.shape["dp"]

    def on_device(
        activations, gradients, basis_in, basis_out, eigen_in, eigen_out, query_in, query_out
    ):
        g, d = lax.axis_index("groups"), lax.axis_index("dp")
        rows = query_in.shape[0] // groups
        tokens = activations.shape[0]
        n_in, n_out = basis_in.shape[0], basis_out.shape[0]
        blocks, width, cols = n_in + n_out, basis_in.shape[1], basis_in.shape[2]

        def mine(query, count):
            part = lax.dynamic_slice_in_dim(query, g * rows, rows, 0)
            return part.reshape(rows, count, dp, cols)

        sent = jnp.concatenate([mine(query_in, n_in), mine(query_out, n_out)], 1)
        got = lax.all_to_all(sent.transpose(2, 0, 1, 3), "dp", 0, 0)
        eigen = jnp.concatenate([eigen_in, eigen_out], 0)
        scale = 1.0 / jnp.sqrt(lax.dynamic_slice_in_dim(eigen, d * cols, cols, 1) + damping)
        weighted = got.reshape(dp * rows, blocks, cols).astype(jnp.float32) * scale[None]
        both = jnp.concatenate(split(weighted), 0)

        def back(basis, w):
            y = jnp.einsum("qbj,bij->qbi", w, basis, preferred_element_type=jnp.float32)
            return y[: dp * rows] + y[dp * rows :]

        partial = jnp.concatenate(
            [back(basis_in, both[:, :n_in]), back(basis_out, both[:, n_in:])], 1
        )
        codes = swap_rows(encode(partial.reshape(dp, rows, blocks, width)), mesh)
        bounds = codes[..., blocks * width : blocks * width + blocks].astype(jnp.float32)
        parts = codes[..., : blocks * width].reshape(dp, rows, blocks, width)
        own = jnp.sum(decode(parts, bounds[..., None]), axis=0)
        full = gather_rows(encode(own), mesh)
        total = groups * dp * rows
        full = full.reshape(total, -1)
        part_in = project(activations, full, 0, n_in, blocks)
        part_out = project(gradients, full, n_in, n_out, blocks)
        products = product(part_in, part_out, mesh).reshape(tokens, groups, dp, rows).transpose(0, 2, 1, 3)
        return jnp.sum(products.reshape(tokens, total // FACTORS, FACTORS), axis=2)

    return on_device


def solution(mesh):
    placed = (
        P(("groups", "dp"), "tensor"),
        P(("groups", "dp"), "tensor"),
        P("tensor", None, "dp"),
        P("tensor", None, "dp"),
        P("tensor", None),
        P("tensor", None),
        P("dp", "tensor"),
        P("dp", "tensor"),
    )
    return jax.shard_map(
        make(mesh), mesh=mesh, in_specs=placed, out_specs=P(("groups", "dp"), None), check_vma=False
    )
```

```python
import functools

import jax
import jax.numpy as jnp
from jax import lax
from jax.experimental import pallas as pl
from jax.experimental.pallas import tpu as pltpu
from jax.sharding import PartitionSpec as P

FACTORS = 4
LANES = 128
damping = 0.1

SPAN = 240.0


def split(x):
    hi = lax.reduce_precision(x, 8, 7)
    return hi.astype(jnp.bfloat16), (x - hi).astype(jnp.bfloat16)


def decode(code, bound):
    c = code.astype(jnp.float32)
    size = (jnp.log2(jnp.abs(c)) + SPAN / 2) * (bound * (1.0 / SPAN))
    return jnp.where(c < 0, -size, size)


def project_kernel(first, x_ref, code_ref, bound_ref, out_ref):
    b = pl.program_id(0)
    bounds = bound_ref[...].astype(jnp.float32)
    lane = lax.broadcasted_iota(jnp.int32, bounds.shape, 1)
    bound = jnp.sum(jnp.where(lane == b + first, bounds, 0.0), axis=1, keepdims=True)
    value = decode(code_ref[...], bound)
    hi = value.astype(jnp.bfloat16)
    lo = (value - hi.astype(jnp.float32)).astype(jnp.bfloat16)
    y = lax.dot_general(
        x_ref[...],
        jnp.concatenate([hi, lo], axis=0),
        (((1,), (1,)), ((), ())),
        preferred_element_type=jnp.float32,
    )
    total = code_ref.shape[0]
    y = y[:, :total] + y[:, total:]

    @pl.when(b == 0)
    def _():
        out_ref[...] = y

    @pl.when(b > 0)
    def _():
        out_ref[...] += y


def project(x, codes, first, blocks, all_blocks):
    tokens, width = x.shape[0], x.shape[1] // blocks
    total = codes.shape[0]
    return pl.pallas_call(
        functools.partial(project_kernel, first),
        grid=(blocks,),
        out_shape=jax.ShapeDtypeStruct((tokens, total), jnp.float32),
        in_specs=[
            pl.BlockSpec((tokens, width), lambda b: (0, b)),
            pl.BlockSpec((total, width), lambda b: (0, b + first)),
            pl.BlockSpec((total, LANES), lambda b: (0, all_blocks * width // LANES)),
        ],
        out_specs=pl.BlockSpec((tokens, total), lambda b: (0, 0)),
        cost_estimate=pl.CostEstimate(
            flops=4 * tokens * total * width * blocks,
            bytes_accessed=2 * (tokens + total) * width * blocks,
            transcendentals=total * width * blocks,
        ),
    )(x, codes, codes)


MESH = pl.DeviceIdType.MESH


def greet(dp):
    g, d, t = (lax.axis_index(n) for n in ("groups", "dp", "tensor"))
    barrier = pltpu.get_barrier_semaphore()
    for k in range(1, dp):
        pl.semaphore_signal(barrier, inc=1, device_id=(g, (d + k) % dp, t), device_id_type=MESH)
    return barrier


def swap(dp, src_ref, dst_ref, local_sem, send_sem, recv_sem):
    g, d, t = (lax.axis_index(n) for n in ("groups", "dp", "tensor"))
    copies = []
    for k in range(1, dp):
        e = (d + k) % dp
        copy = pltpu.make_async_remote_copy(
            src_ref=src_ref.at[e],
            dst_ref=dst_ref.at[d],
            send_sem=send_sem.at[k],
            recv_sem=recv_sem.at[k],
            device_id=(g, e, t),
            device_id_type=MESH,
        )
        copy.start()
        copies.append(copy)
    local = pltpu.make_async_copy(src_ref.at[d], dst_ref.at[d], local_sem)
    local.start()
    local.wait()
    for copy in copies:
        copy.wait()


def swap_sems(dp):
    return [
        pltpu.SemaphoreType.DMA,
        pltpu.SemaphoreType.DMA((dp,)),
        pltpu.SemaphoreType.DMA((dp,)),
    ]


def query_kernel(dp, src_ref, dst_ref, local_sem, send_sem, recv_sem):
    pl.semaphore_wait(greet(dp), dp - 1)
    swap(dp, src_ref, dst_ref, local_sem, send_sem, recv_sem)


def swap_queries(sent):
    vmem = pl.BlockSpec(memory_space=pltpu.VMEM)
    return pl.pallas_call(
        functools.partial(query_kernel, sent.shape[0]),
        out_shape=jax.ShapeDtypeStruct(sent.shape, sent.dtype),
        in_specs=[vmem],
        out_specs=vmem,
        scratch_shapes=swap_sems(sent.shape[0]),
        compiler_params=pltpu.CompilerParams(collective_id=2, has_side_effects=True),
    )(sent)


def encode_block(x):
    bound = jnp.maximum(jnp.max(jnp.abs(x), axis=1, keepdims=True), 1e-30) * 1.01
    bound = bound.astype(jnp.bfloat16).astype(jnp.float32)
    y = jnp.exp2(jnp.abs(x) * (SPAN / bound) - SPAN / 2)
    return jnp.where(x < 0, -y, y), bound


def reduce_kernel(dp, w_ref, in_ref, out_basis_ref, own_ref, code, held, *sems):
    barrier = greet(dp)
    n_in, n_out = in_ref.shape[0], out_basis_ref.shape[0]
    width = in_ref.shape[1]
    blocks, rows = n_in + n_out, own_ref.shape[0]
    end = blocks * width
    tail = jnp.zeros((dp * rows, LANES), jnp.float32)
    lane = lax.broadcasted_iota(jnp.int32, tail.shape, 1)
    for b in range(blocks):
        basis = in_ref[b] if b < n_in else out_basis_ref[b - n_in]
        y = lax.dot_general(
            w_ref[b], basis, (((1,), (1,)), ((), ())), preferred_element_type=jnp.float32
        )
        c, bound = encode_block(y[: dp * rows] + y[dp * rows :])
        tail = jnp.where(lane == b, bound, tail)
        for e in range(dp):
            code[e, :, b * width : (b + 1) * width] = c[e * rows : (e + 1) * rows].astype(jnp.bfloat16)
    for e in range(dp):
        code[e, :, end:] = tail[e * rows : (e + 1) * rows].astype(jnp.bfloat16)
    pl.semaphore_wait(barrier, dp - 1)
    swap(dp, code, held, *sems)
    bounds = [held[e, :, end:].astype(jnp.float32) for e in range(dp)]
    tail = jnp.zeros((rows, LANES), jnp.float32)
    lane = lax.broadcasted_iota(jnp.int32, tail.shape, 1)
    for b in range(blocks):
        cols = slice(b * width, (b + 1) * width)
        total = decode(held[0, :, cols], bounds[0][:, b : b + 1])
        for e in range(1, dp):
            total = total + decode(held[e, :, cols], bounds[e][:, b : b + 1])
        c, bound = encode_block(total)
        tail = jnp.where(lane == b, bound, tail)
        own_ref[:, cols] = c.astype(jnp.bfloat16)
    own_ref[:, end:] = tail.astype(jnp.bfloat16)


def reduce_rows(w, basis_in, basis_out, dp, rows):
    length = w.shape[0] * basis_in.shape[1] + LANES
    vmem = pl.BlockSpec(memory_space=pltpu.VMEM)
    return pl.pallas_call(
        functools.partial(reduce_kernel, dp),
        out_shape=jax.ShapeDtypeStruct((rows, length), jnp.bfloat16),
        in_specs=[vmem] * 3,
        out_specs=vmem,
        scratch_shapes=[pltpu.VMEM((dp, rows, length), jnp.bfloat16)] * 2 + swap_sems(dp),
        compiler_params=pltpu.CompilerParams(collective_id=3, has_side_effects=True),
    )(w, basis_in, basis_out)


def gather_kernel(groups, lines, pairs, own_ref, out_ref, local_sem, send_sem, recv_sem):
    g, d = lax.axis_index("groups"), lax.axis_index("dp")
    t = lax.axis_index("tensor")
    a, b = d // pairs, d % pairs
    length = own_ref.shape[1]
    middle = (length // LANES + 1) // 2 * LANES
    halves = (pl.ds(0, middle), pl.ds(middle, length - middle))
    order = [k for pair in zip(range(1, lines), range(lines - 1, 0, -1)) for k in pair]
    order = list(dict.fromkeys(order))
    line_peers = [(g, (a + k) % lines * pairs + b, t) for k in order]
    pair_peers = [(g, a * pairs + (b + k) % pairs, t) for k in range(1, pairs)]
    group_peers = [((g + k) % groups, d, t) for k in range(1, groups)]
    other_b = [(b + k) % pairs for k in range(1, pairs)]
    other_g = [(g + k) % groups for k in range(1, groups)]

    barrier = pltpu.get_barrier_semaphore()
    peers = line_peers + pair_peers + group_peers
    for peer in peers:
        pl.semaphore_signal(barrier, inc=1, device_id=peer, device_id_type=MESH)
    pl.semaphore_wait(barrier, len(peers))

    started = []

    def send(pg, pd, half, peer, own=False):
        src = own_ref.at[:, halves[half]] if own else out_ref.at[pg, pd, :, halves[half]]
        copy = pltpu.make_async_remote_copy(
            src_ref=src,
            dst_ref=out_ref.at[pg, pd, :, halves[half]],
            send_sem=send_sem.at[len(started)],
            recv_sem=recv_sem.at[pg, pd, half],
            device_id=peer,
            device_id_type=MESH,
        )
        copy.start()
        started.append(copy)

    def arrived(pg, pd, half):
        here = out_ref.at[pg, pd, :, halves[half]]
        pltpu.make_async_remote_copy(
            src_ref=here,
            dst_ref=here,
            send_sem=send_sem.at[0],
            recv_sem=recv_sem.at[pg, pd, half],
            device_id=peers[0],
            device_id_type=MESH,
        ).wait_recv()

    def across(pa):
        for ob in other_b:
            arrived(g, pa * pairs + ob, 0)
            for peer in group_peers:
                send(g, pa * pairs + ob, 0, peer)
        for og in other_g:
            arrived(og, pa * pairs + b, 1)
            for peer in pair_peers:
                send(og, pa * pairs + b, 1, peer)

    for half in (0, 1):
        for peer in line_peers:
            send(g, d, half, peer, True)
        for peer in pair_peers + group_peers:
            send(g, d, half, peer, True)
    local = pltpu.make_async_copy(own_ref, out_ref.at[g, d], local_sem)
    local.start()
    places = [a] + [(a - k) % lines for k in order]
    for i, pa in enumerate(places):
        if i > 0:
            for half in (0, 1):
                arrived(g, pa * pairs + b, half)
                for peer in pair_peers + group_peers:
                    send(g, pa * pairs + b, half, peer)
            across(places[i - 1])
    across(places[-1])
    for pa in places:
        for ob in other_b:
            arrived(g, pa * pairs + ob, 1)
        for og in other_g:
            arrived(og, pa * pairs + b, 0)
            for ob in other_b:
                for half in (0, 1):
                    arrived(og, pa * pairs + ob, half)
    local.wait()
    for copy in started:
        copy.wait_send()


def gather_rows(own, mesh):
    groups, dp = mesh.shape["groups"], mesh.shape["dp"]
    pairs = 2 if dp % 2 == 0 else 1
    lines = dp // pairs
    cross = (pairs - 1) + (groups - 1)
    sends = 2 * (lines - 1) + 2 * lines * cross + 2 * lines * (pairs - 1) * (groups - 1)
    vmem = pl.BlockSpec(memory_space=pltpu.VMEM)
    return pl.pallas_call(
        functools.partial(gather_kernel, groups, lines, pairs),
        out_shape=jax.ShapeDtypeStruct((groups, dp, *own.shape), own.dtype),
        in_specs=[vmem],
        out_specs=vmem,
        scratch_shapes=[
            pltpu.SemaphoreType.DMA,
            pltpu.SemaphoreType.DMA((sends,)),
            pltpu.SemaphoreType.DMA((groups, dp, 2)),
        ],
        compiler_params=pltpu.CompilerParams(collective_id=0, has_side_effects=True),
    )(own)


def product_kernel(in_ref, out_part_ref, prod_ref, held, send_sem, recv_sem):
    other = (lax.axis_index("groups"), lax.axis_index("dp"), 1 - lax.axis_index("tensor"))
    barrier = pltpu.get_barrier_semaphore()
    pl.semaphore_signal(barrier, inc=1, device_id=other, device_id_type=MESH)
    pl.semaphore_wait(barrier, 1)
    copies = []
    for i, ref in enumerate((in_ref, out_part_ref)):
        copy = pltpu.make_async_remote_copy(
            src_ref=ref,
            dst_ref=held.at[i],
            send_sem=send_sem.at[i],
            recv_sem=recv_sem.at[i],
            device_id=other,
            device_id_type=MESH,
        )
        copy.start()
        copies.append(copy)
    for copy in copies:
        copy.wait()
    prod_ref[...] = (in_ref[...] + held[0]) * (out_part_ref[...] + held[1])


def product(part_in, part_out, mesh):
    if mesh.shape["tensor"] != 2:
        part_in, part_out = lax.psum((part_in, part_out), "tensor")
        return part_in * part_out
    vmem = pl.BlockSpec(memory_space=pltpu.VMEM)
    return pl.pallas_call(
        product_kernel,
        out_shape=jax.ShapeDtypeStruct(part_in.shape, part_in.dtype),
        in_specs=[vmem, vmem],
        out_specs=vmem,
        scratch_shapes=[
            pltpu.VMEM((2, *part_in.shape), part_in.dtype),
            pltpu.SemaphoreType.DMA((2,)),
            pltpu.SemaphoreType.DMA((2,)),
        ],
        compiler_params=pltpu.CompilerParams(collective_id=1, has_side_effects=True),
    )(part_in, part_out)


def make(mesh):
    groups, dp = mesh.shape["groups"], mesh.shape["dp"]

    def on_device(
        activations, gradients, basis_in, basis_out, eigen_in, eigen_out, query_in, query_out
    ):
        g, d = lax.axis_index("groups"), lax.axis_index("dp")
        rows = query_in.shape[0] // groups
        tokens = activations.shape[0]
        n_in, n_out = basis_in.shape[0], basis_out.shape[0]
        blocks, width, cols = n_in + n_out, basis_in.shape[1], basis_in.shape[2]

        def mine(query, count):
            part = lax.dynamic_slice_in_dim(query, g * rows, rows, 0)
            return part.reshape(rows, count, dp, cols)

        sent = jnp.concatenate([mine(query_in, n_in), mine(query_out, n_out)], 1)
        got = swap_queries(sent.transpose(2, 1, 0, 3).reshape(dp, blocks * rows, cols))
        got = got.reshape(dp, blocks, rows, cols)
        eigen = jnp.concatenate([eigen_in, eigen_out], 0)
        scale = 1.0 / jnp.sqrt(lax.dynamic_slice_in_dim(eigen, d * cols, cols, 1) + damping)
        weighted = got.astype(jnp.float32) * scale[None, :, None]
        weighted = weighted.transpose(1, 0, 2, 3).reshape(blocks, dp * rows, cols)
        both = jnp.concatenate(split(weighted), 1)
        own = reduce_rows(both, basis_in, basis_out, dp, rows)
        full = gather_rows(own, mesh)
        total = groups * dp * rows
        full = full.reshape(total, -1)
        part_in = project(activations, full, 0, n_in, blocks)
        part_out = project(gradients, full, n_in, n_out, blocks)
        products = product(part_in, part_out, mesh).reshape(tokens, groups, dp, rows).transpose(0, 2, 1, 3)
        return jnp.sum(products.reshape(tokens, total // FACTORS, FACTORS), axis=2)

    return on_device


def solution(mesh):
    placed = (
        P(("groups", "dp"), "tensor"),
        P(("groups", "dp"), "tensor"),
        P("tensor", None, "dp"),
        P("tensor", None, "dp"),
        P("tensor", None),
        P("tensor", None),
        P("dp", "tensor"),
        P("dp", "tensor"),
    )
    return jax.shard_map(
        make(mesh), mesh=mesh, in_specs=placed, out_specs=P(("groups", "dp"), None), check_vma=False
    )
```

```python
import functools

import jax
import jax.numpy as jnp
from jax import lax
from jax.experimental import pallas as pl
from jax.experimental.pallas import tpu as pltpu
from jax.sharding import PartitionSpec as P

FACTORS = 4
LANES = 128
damping = 0.1

SPAN = 240.0


def decode(code, bound):
    c = code.astype(jnp.float32)
    size = (jnp.log2(jnp.abs(c)) + SPAN / 2) * (bound * (1.0 / SPAN))
    return jnp.where(c < 0, -size, size)


def project_kernel(first, x_ref, code_ref, bound_ref, out_ref):
    b = pl.program_id(0)
    bounds = bound_ref[...].astype(jnp.float32)
    lane = lax.broadcasted_iota(jnp.int32, bounds.shape, 1)
    bound = jnp.sum(jnp.where(lane == b + first, bounds, 0.0), axis=1, keepdims=True)
    value = decode(code_ref[...], bound)
    hi = value.astype(jnp.bfloat16)
    lo = (value - hi.astype(jnp.float32)).astype(jnp.bfloat16)
    y = lax.dot_general(
        x_ref[...],
        jnp.concatenate([hi, lo], axis=0),
        (((1,), (1,)), ((), ())),
        preferred_element_type=jnp.float32,
    )
    total = code_ref.shape[0]
    y = y[:, :total] + y[:, total:]

    @pl.when(b == 0)
    def _():
        out_ref[...] = y

    @pl.when(b > 0)
    def _():
        out_ref[...] += y


def project(x, codes, first, blocks, all_blocks):
    tokens, width = x.shape[0], x.shape[1] // blocks
    total = codes.shape[0]
    return pl.pallas_call(
        functools.partial(project_kernel, first),
        grid=(blocks,),
        out_shape=jax.ShapeDtypeStruct((tokens, total), jnp.float32),
        in_specs=[
            pl.BlockSpec((tokens, width), lambda b: (0, b)),
            pl.BlockSpec((total, width), lambda b: (0, b + first)),
            pl.BlockSpec((total, LANES), lambda b: (0, all_blocks * width // LANES)),
        ],
        out_specs=pl.BlockSpec((tokens, total), lambda b: (0, 0)),
        cost_estimate=pl.CostEstimate(
            flops=4 * tokens * total * width * blocks,
            bytes_accessed=2 * (tokens + total) * width * blocks,
            transcendentals=total * width * blocks,
        ),
    )(x, codes, codes)


MESH = pl.DeviceIdType.MESH


def greet(dp):
    g, d, t = (lax.axis_index(n) for n in ("groups", "dp", "tensor"))
    barrier = pltpu.get_barrier_semaphore()
    for k in range(1, dp):
        pl.semaphore_signal(barrier, inc=1, device_id=(g, (d + k) % dp, t), device_id_type=MESH)
    return barrier


def swap(dp, src_ref, dst_ref, local_sem, send_sem, recv_sem):
    g, d, t = (lax.axis_index(n) for n in ("groups", "dp", "tensor"))
    copies = []
    for k in range(1, dp):
        e = (d + k) % dp
        copy = pltpu.make_async_remote_copy(
            src_ref=src_ref.at[e],
            dst_ref=dst_ref.at[d],
            send_sem=send_sem.at[k],
            recv_sem=recv_sem.at[k],
            device_id=(g, e, t),
            device_id_type=MESH,
        )
        copy.start()
        copies.append(copy)
    local = pltpu.make_async_copy(src_ref.at[d], dst_ref.at[d], local_sem)
    local.start()
    local.wait()
    for copy in copies:
        copy.wait()


def swap_sems(dp):
    return [
        pltpu.SemaphoreType.DMA,
        pltpu.SemaphoreType.DMA((dp,)),
        pltpu.SemaphoreType.DMA((dp,)),
    ]


def query_kernel(dp, src_ref, dst_ref, local_sem, send_sem, recv_sem):
    pl.semaphore_wait(greet(dp), dp - 1)
    swap(dp, src_ref, dst_ref, local_sem, send_sem, recv_sem)


def swap_queries(sent):
    vmem = pl.BlockSpec(memory_space=pltpu.VMEM)
    return pl.pallas_call(
        functools.partial(query_kernel, sent.shape[0]),
        out_shape=jax.ShapeDtypeStruct(sent.shape, sent.dtype),
        in_specs=[vmem],
        out_specs=vmem,
        scratch_shapes=swap_sems(sent.shape[0]),
        compiler_params=pltpu.CompilerParams(collective_id=2, has_side_effects=True),
    )(sent)


def encode_block(x):
    bound = jnp.maximum(jnp.max(jnp.abs(x), axis=1, keepdims=True), 1e-30) * 1.01
    bound = bound.astype(jnp.bfloat16).astype(jnp.float32)
    y = jnp.exp2(jnp.abs(x) * (SPAN / bound) - SPAN / 2)
    return jnp.where(x < 0, -y, y), bound


def reduce_kernel(dp, query_ref, scale_ref, in_ref, out_basis_ref, own_ref, code, held, *sems):
    barrier = greet(dp)
    n_in, n_out = in_ref.shape[0], out_basis_ref.shape[0]
    width = in_ref.shape[1]
    blocks, rows = n_in + n_out, own_ref.shape[0]
    end = blocks * width
    tail = jnp.zeros((dp * rows, LANES), jnp.float32)
    lane = lax.broadcasted_iota(jnp.int32, tail.shape, 1)
    for b in range(blocks):
        basis = in_ref[b] if b < n_in else out_basis_ref[b - n_in]
        w = jnp.concatenate(
            [query_ref[e, b * rows : (b + 1) * rows, :].astype(jnp.float32) for e in range(dp)], axis=0
        )
        w = w * scale_ref[b : b + 1, :]
        hi = w.astype(jnp.bfloat16)
        lo = (w - hi.astype(jnp.float32)).astype(jnp.bfloat16)
        y = lax.dot_general(
            jnp.concatenate([hi, lo], axis=0), basis, (((1,), (1,)), ((), ())), preferred_element_type=jnp.float32
        )
        c, bound = encode_block(y[: dp * rows] + y[dp * rows :])
        tail = jnp.where(lane == b, bound, tail)
        for e in range(dp):
            code[e, :, b * width : (b + 1) * width] = c[e * rows : (e + 1) * rows].astype(jnp.bfloat16)
    for e in range(dp):
        code[e, :, end:] = tail[e * rows : (e + 1) * rows].astype(jnp.bfloat16)
    pl.semaphore_wait(barrier, dp - 1)
    swap(dp, code, held, *sems)
    bounds = [held[e, :, end:].astype(jnp.float32) for e in range(dp)]
    tail = jnp.zeros((rows, LANES), jnp.float32)
    lane = lax.broadcasted_iota(jnp.int32, tail.shape, 1)
    for b in range(blocks):
        cols = slice(b * width, (b + 1) * width)
        total = decode(held[0, :, cols], bounds[0][:, b : b + 1])
        for e in range(1, dp):
            total = total + decode(held[e, :, cols], bounds[e][:, b : b + 1])
        c, bound = encode_block(total)
        tail = jnp.where(lane == b, bound, tail)
        own_ref[:, cols] = c.astype(jnp.bfloat16)
    own_ref[:, end:] = tail.astype(jnp.bfloat16)


def reduce_rows(queries, scale, basis_in, basis_out, dp, rows):
    length = scale.shape[0] * basis_in.shape[1] + LANES
    vmem = pl.BlockSpec(memory_space=pltpu.VMEM)
    return pl.pallas_call(
        functools.partial(reduce_kernel, dp),
        out_shape=jax.ShapeDtypeStruct((rows, length), jnp.bfloat16),
        in_specs=[vmem] * 4,
        out_specs=vmem,
        scratch_shapes=[pltpu.VMEM((dp, rows, length), jnp.bfloat16)] * 2 + swap_sems(dp),
        compiler_params=pltpu.CompilerParams(collective_id=3, has_side_effects=True),
    )(queries, scale, basis_in, basis_out)


def gather_kernel(groups, lines, pairs, own_ref, out_ref, local_sem, send_sem, recv_sem):
    g, d = lax.axis_index("groups"), lax.axis_index("dp")
    t = lax.axis_index("tensor")
    a, b = d // pairs, d % pairs
    length = own_ref.shape[1]
    middle = (length // LANES + 1) // 2 * LANES
    halves = (pl.ds(0, middle), pl.ds(middle, length - middle))
    order = [k for pair in zip(range(1, lines), range(lines - 1, 0, -1)) for k in pair]
    order = list(dict.fromkeys(order))
    line_peers = [(g, (a + k) % lines * pairs + b, t) for k in order]
    pair_peers = [(g, a * pairs + (b + k) % pairs, t) for k in range(1, pairs)]
    group_peers = [((g + k) % groups, d, t) for k in range(1, groups)]
    other_b = [(b + k) % pairs for k in range(1, pairs)]
    other_g = [(g + k) % groups for k in range(1, groups)]

    barrier = pltpu.get_barrier_semaphore()
    peers = line_peers + pair_peers + group_peers
    for peer in peers:
        pl.semaphore_signal(barrier, inc=1, device_id=peer, device_id_type=MESH)
    pl.semaphore_wait(barrier, len(peers))

    started = []

    def send(pg, pd, half, peer, own=False):
        src = own_ref.at[:, halves[half]] if own else out_ref.at[pg, pd, :, halves[half]]
        copy = pltpu.make_async_remote_copy(
            src_ref=src,
            dst_ref=out_ref.at[pg, pd, :, halves[half]],
            send_sem=send_sem.at[len(started)],
            recv_sem=recv_sem.at[pg, pd, half],
            device_id=peer,
            device_id_type=MESH,
        )
        copy.start()
        started.append(copy)

    def arrived(pg, pd, half):
        here = out_ref.at[pg, pd, :, halves[half]]
        pltpu.make_async_remote_copy(
            src_ref=here,
            dst_ref=here,
            send_sem=send_sem.at[0],
            recv_sem=recv_sem.at[pg, pd, half],
            device_id=peers[0],
            device_id_type=MESH,
        ).wait_recv()

    def across(pa):
        for ob in other_b:
            arrived(g, pa * pairs + ob, 0)
            for peer in group_peers:
                send(g, pa * pairs + ob, 0, peer)
        for og in other_g:
            arrived(og, pa * pairs + b, 1)
            for peer in pair_peers:
                send(og, pa * pairs + b, 1, peer)

    for half in (0, 1):
        for peer in line_peers:
            send(g, d, half, peer, True)
        for peer in pair_peers + group_peers:
            send(g, d, half, peer, True)
    local = pltpu.make_async_copy(own_ref, out_ref.at[g, d], local_sem)
    local.start()
    places = [a] + [(a - k) % lines for k in order]
    for i, pa in enumerate(places):
        if i > 0:
            for half in (0, 1):
                arrived(g, pa * pairs + b, half)
                for peer in pair_peers + group_peers:
                    send(g, pa * pairs + b, half, peer)
            across(places[i - 1])
    across(places[-1])
    for pa in places:
        for ob in other_b:
            arrived(g, pa * pairs + ob, 1)
        for og in other_g:
            arrived(og, pa * pairs + b, 0)
            for ob in other_b:
                for half in (0, 1):
                    arrived(og, pa * pairs + ob, half)
    local.wait()
    for copy in started:
        copy.wait_send()


def gather_rows(own, mesh):
    groups, dp = mesh.shape["groups"], mesh.shape["dp"]
    pairs = 2 if dp % 2 == 0 else 1
    lines = dp // pairs
    cross = (pairs - 1) + (groups - 1)
    sends = 2 * (lines - 1) + 2 * lines * cross + 2 * lines * (pairs - 1) * (groups - 1)
    vmem = pl.BlockSpec(memory_space=pltpu.VMEM)
    return pl.pallas_call(
        functools.partial(gather_kernel, groups, lines, pairs),
        out_shape=jax.ShapeDtypeStruct((groups, dp, *own.shape), own.dtype),
        in_specs=[vmem],
        out_specs=vmem,
        scratch_shapes=[
            pltpu.SemaphoreType.DMA,
            pltpu.SemaphoreType.DMA((sends,)),
            pltpu.SemaphoreType.DMA((groups, dp, 2)),
        ],
        compiler_params=pltpu.CompilerParams(collective_id=0, has_side_effects=True),
    )(own)


def product_kernel(in_ref, out_part_ref, prod_ref, held, send_sem, recv_sem):
    other = (lax.axis_index("groups"), lax.axis_index("dp"), 1 - lax.axis_index("tensor"))
    barrier = pltpu.get_barrier_semaphore()
    pl.semaphore_signal(barrier, inc=1, device_id=other, device_id_type=MESH)
    pl.semaphore_wait(barrier, 1)
    copies = []
    for i, ref in enumerate((in_ref, out_part_ref)):
        copy = pltpu.make_async_remote_copy(
            src_ref=ref,
            dst_ref=held.at[i],
            send_sem=send_sem.at[i],
            recv_sem=recv_sem.at[i],
            device_id=other,
            device_id_type=MESH,
        )
        copy.start()
        copies.append(copy)
    for copy in copies:
        copy.wait()
    prod_ref[...] = (in_ref[...] + held[0]) * (out_part_ref[...] + held[1])


def product(part_in, part_out, mesh):
    if mesh.shape["tensor"] != 2:
        part_in, part_out = lax.psum((part_in, part_out), "tensor")
        return part_in * part_out
    vmem = pl.BlockSpec(memory_space=pltpu.VMEM)
    return pl.pallas_call(
        product_kernel,
        out_shape=jax.ShapeDtypeStruct(part_in.shape, part_in.dtype),
        in_specs=[vmem, vmem],
        out_specs=vmem,
        scratch_shapes=[
            pltpu.VMEM((2, *part_in.shape), part_in.dtype),
            pltpu.SemaphoreType.DMA((2,)),
            pltpu.SemaphoreType.DMA((2,)),
        ],
        compiler_params=pltpu.CompilerParams(collective_id=1, has_side_effects=True),
    )(part_in, part_out)


def make(mesh):
    groups, dp = mesh.shape["groups"], mesh.shape["dp"]

    def on_device(
        activations, gradients, basis_in, basis_out, eigen_in, eigen_out, query_in, query_out
    ):
        g, d = lax.axis_index("groups"), lax.axis_index("dp")
        rows = query_in.shape[0] // groups
        tokens = activations.shape[0]
        n_in, n_out = basis_in.shape[0], basis_out.shape[0]
        blocks, width, cols = n_in + n_out, basis_in.shape[1], basis_in.shape[2]

        def mine(query, count):
            part = lax.dynamic_slice_in_dim(query, g * rows, rows, 0)
            return part.reshape(rows, count, dp, cols)

        sent = jnp.concatenate([mine(query_in, n_in), mine(query_out, n_out)], 1)
        got = swap_queries(sent.transpose(2, 1, 0, 3).reshape(dp, blocks * rows, cols))
        eigen = jnp.concatenate([eigen_in, eigen_out], 0)
        scale = 1.0 / jnp.sqrt(lax.dynamic_slice_in_dim(eigen, d * cols, cols, 1) + damping)
        own = reduce_rows(got, scale, basis_in, basis_out, dp, rows)
        full = gather_rows(own, mesh)
        total = groups * dp * rows
        full = full.reshape(total, -1)
        part_in = project(activations, full, 0, n_in, blocks)
        part_out = project(gradients, full, n_in, n_out, blocks)
        products = product(part_in, part_out, mesh).reshape(tokens, groups, dp, rows).transpose(0, 2, 1, 3)
        return jnp.sum(products.reshape(tokens, total // FACTORS, FACTORS), axis=2)

    return on_device


def solution(mesh):
    placed = (
        P(("groups", "dp"), "tensor"),
        P(("groups", "dp"), "tensor"),
        P("tensor", None, "dp"),
        P("tensor", None, "dp"),
        P("tensor", None),
        P("tensor", None),
        P("dp", "tensor"),
        P("dp", "tensor"),
    )
    return jax.shard_map(
        make(mesh), mesh=mesh, in_specs=placed, out_specs=P(("groups", "dp"), None), check_vma=False
    )
```
